32 devices in a mesh: seq: 8 (over y, x, core), fsdp: 4 (over z).
Axes of the slice: x: 2, y: 2, z: 4, core: 2. Of those that a mesh axis runs over, the one named last changes fastest.
Arguments:
- tokens: bfloat16 [12, 1376, 1024], P('fsdp', 'seq'), may hold values from -16 to 16
- cotangent: bfloat16 [12, 1376, 1024], P('fsdp', 'seq'), may hold values from -6 to 6
- lengths: int32 [12], P('fsdp'), may hold values from 688 to 1370, as said below
- joint_weight: bfloat16 [1024, 3072], P(('seq', 'fsdp')), may hold values from -6 to 6
- output_weight: bfloat16 [1024, 1024], P(('seq', 'fsdp')), may hold values from -1.5 to 1.5
- expand_weight: bfloat16 [1024, 4096], P(('seq', 'fsdp')), may hold values from -0.1875 to 0.1875
- reduce_weight: bfloat16 [4096, 1024], P(('seq', 'fsdp')), may hold values from -0.09375 to 0.09375
- vectors: bfloat16 [10, 1024], P(None, ('seq', 'fsdp')), may hold values from -1.7 to 1.8
- expand_bias: bfloat16 [4096], P(('seq', 'fsdp')), may hold values from -0.59765625 to 0.59765625
- first_joint: float32 [1024, 3072], P(('seq', 'fsdp')), may hold values from -46.25965 to 46.25965
- first_output: float32 [1024, 1024], P(('seq', 'fsdp')), may hold values from -7.709942 to 7.709942
- first_expand: float32 [1024, 4096], P(('seq', 'fsdp')), may hold values from -23.129826 to 23.129826
- first_reduce: float32 [4096, 1024], P(('seq', 'fsdp')), may hold values from -46.25965 to 46.25965
- first_vectors: float32 [10, 1024], P(None, ('seq', 'fsdp')), may hold values from -77.09942 to 77.09942
- first_bias: float32 [4096], P(('seq', 'fsdp')), may hold values from -23.129826 to 23.129826
- second_joint: float32 [1024, 3072], P(('seq', 'fsdp')), may hold values from 1.6512 to 16.512
- second_output: float32 [1024, 1024], P(('seq', 'fsdp')), may hold values from 0.049536 to 0.49536
- second_expand: float32 [1024, 4096], P(('seq', 'fsdp')), may hold values from 0.49536 to 4.9536
- second_reduce: float32 [4096, 1024], P(('seq', 'fsdp')), may hold values from 1.6512 to 16.512
- second_vectors: float32 [10, 1024], P(None, ('seq', 'fsdp')), may hold values from 4.9536 to 49.536
- second_bias: float32 [4096], P(('seq', 'fsdp')), may hold values from 0.49536 to 4.9536
Outputs:
- block_output: bfloat16 [12, 1376, 1024], P('fsdp', 'seq')
- input_grad: bfloat16 [12, 1376, 1024], P('fsdp', 'seq')
- joint_grad: float32 [1024, 3072], P(('seq', 'fsdp'))
- output_grad: float32 [1024, 1024], P(('seq', 'fsdp'))
- expand_grad: float32 [1024, 4096], P(('seq', 'fsdp'))
- reduce_grad: float32 [4096, 1024], P(('seq', 'fsdp'))
- vector_grad: float32 [10, 1024], P(None, ('seq', 'fsdp'))
- bias_grad: float32 [4096], P(('seq', 'fsdp'))
- joint_new: float32 [1024, 3072], P(('seq', 'fsdp'))
- output_new: float32 [1024, 1024], P(('seq', 'fsdp'))
- expand_new: float32 [1024, 4096], P(('seq', 'fsdp'))
- reduce_new: float32 [4096, 1024], P(('seq', 'fsdp'))
- vector_new: float32 [10, 1024], P(None, ('seq', 'fsdp'))
- bias_new: float32 [4096], P(('seq', 'fsdp'))
- mean_joint: float32 [1024, 3072], P(('seq', 'fsdp'))
- mean_output: float32 [1024, 1024], P(('seq', 'fsdp'))
- mean_expand: float32 [1024, 4096], P(('seq', 'fsdp'))
- mean_reduce: float32 [4096, 1024], P(('seq', 'fsdp'))
- mean_vectors: float32 [10, 1024], P(None, ('seq', 'fsdp'))
- mean_bias: float32 [4096], P(('seq', 'fsdp'))
- square_joint: float32 [1024, 3072], P(('seq', 'fsdp'))
- square_output: float32 [1024, 1024], P(('seq', 'fsdp'))
- square_expand: float32 [1024, 4096], P(('seq', 'fsdp'))
- square_reduce: float32 [4096, 1024], P(('seq', 'fsdp'))
- square_vectors: float32 [10, 1024], P(None, ('seq', 'fsdp'))
- square_bias: float32 [4096], P(('seq', 'fsdp'))
The draws below stay inside these ranges and needn't reach their ends.
Inputs may be any that keep to these rules, and one draw needn't show every extreme that they name: `lengths`: image 0 has exactly 1370 valid tokens.
All inputs are finite; a program needn't handle non-finite values.
Results may differ from the reference program's by a relative error of at most 0.009.
The reference program's roundings to bfloat16 on the way count: a program that leaves them out, or rounds other values in their place, can miss the bound.
Values may be sent and summed in bfloat16 or wider, within the bound.
No kernel may reach another device: no remote copies, remote signals or barrier semaphores. Data moves between devices by JAX's collectives and lax.ppermute only.
A program may use at most 192 MiB of HBM per device.

```python
import math
import jax
import jax.numpy as jnp
from jax import lax

D = 1024
H = 16
HD = 64
FF = 4096
L = 1376
NVEC = 10
ADAM_STEP = 2
IMAGES = 12
TOKENS = 16512


def draw_tokens(key, part):
    base = jax.random.normal(jax.random.fold_in(key, 11), (IMAGES, L, D), jnp.float32)
    return jnp.clip(base, -16.0, 16.0).astype(jnp.bfloat16)


def draw_lengths(key, part):
    values = jax.random.randint(jax.random.fold_in(key, 21), (IMAGES,), L // 2, L - 5)
    return values.at[0].set(L - 6).astype(jnp.int32)


def draw_joint_weight(key, part):
    base = jnp.clip(jax.random.normal(jax.random.fold_in(key, 31), (D, 3 * D), jnp.float32), -6.0, 6.0) / D ** 0.5
    return jnp.clip(base, -6.0, 6.0).astype(jnp.bfloat16)


def draw_vectors(key, part):
    spread = jnp.clip(jax.random.normal(jax.random.fold_in(key, 41), (NVEC, D), jnp.float32), -4.0, 4.0)
    row_of = jnp.arange(NVEC)[:, None]
    gainlike = (row_of == 0) | (row_of == 5) | (row_of == 6) | (row_of == 9)
    return jnp.where(gainlike, 1.0 + 0.2 * spread, 0.3 * spread).astype(jnp.bfloat16)


def levels(own_key, shape, cuts, smallest, largest):
    loudness = 1.0
    for position, parts in cuts:
        steps = jax.random.uniform(jax.random.fold_in(jax.random.fold_in(own_key, 6), position), (parts,), jnp.float32, smallest / len(cuts), largest / len(cuts))
        loudness = loudness * jnp.repeat(jnp.exp(steps), shape[position] // parts).reshape((-1,) + (1,) * (len(shape) - 1 - position))
    return loudness


def bell_draw(rng, extent, scale, limit, cuts=(), dtype=jnp.bfloat16):
    values = jax.random.normal(rng, extent, jnp.float32) * scale
    if len(cuts) > 0:
        values = levels(rng, extent, cuts, -0.22, 0.18) * values
    return jnp.clip(values, min=-limit, max=limit).astype(dtype)


def setup_inputs(seed: int = 0) -> dict:
    splits = jax.random.split(jax.random.key(seed), 22)
    tokens = draw_tokens(jax.random.fold_in(splits[21], 71), 0)
    cotangent = bell_draw(splits[1], (IMAGES, L, D), 1.0, 6.0, ((0, 4), (1, 8)))
    lengths = draw_lengths(jax.random.fold_in(splits[21], 71), 0)
    joint_weight = draw_joint_weight(jax.random.fold_in(splits[21], 71), 0)
    output_weight = bell_draw(splits[4], (D, D), (D // 64) ** -0.5, 1.5, ((0, 32),))
    expand_weight = bell_draw(splits[5], (D, FF), D ** -0.5, 0.1875, ((0, 32),))
    reduce_weight = bell_draw(splits[6], (FF, D), FF ** -0.5, 0.09375, ((0, 32),))
    vectors = draw_vectors(jax.random.fold_in(splits[21], 71), 0)
    expand_bias = bell_draw(splits[8], (FF,), 0.1, 0.59765625, ((0, 32),))
    first_joint = bell_draw(splits[9], (D, 3 * D), (0.06 * TOKENS ** 0.5), 46.25965, ((0, 32),), jnp.float32)
    first_output = bell_draw(splits[10], (D, D), (0.01 * TOKENS ** 0.5), 7.709942, ((0, 32),), jnp.float32)
    first_expand = bell_draw(splits[11], (D, FF), (0.03 * TOKENS ** 0.5), 23.129826, ((0, 32),), jnp.float32)
    first_reduce = bell_draw(splits[12], (FF, D), (0.06 * TOKENS ** 0.5), 46.25965, ((0, 32),), jnp.float32)
    first_vectors = bell_draw(splits[13], (NVEC, D), (0.1 * TOKENS ** 0.5), 77.09942, ((1, 32),), jnp.float32)
    first_bias = bell_draw(splits[14], (FF,), (0.03 * TOKENS ** 0.5), 23.129826, ((0, 32),), jnp.float32)
    second_joint = jnp.clip(jnp.exp(math.log(16.512) - 2.30258501 * jax.random.uniform(splits[15], (D, 3 * D), jnp.float32) ** levels(splits[15], (D, 3 * D), ((0, 32),), -0.2, 0.2)), 1.6512, 16.512)
    second_output = jnp.clip(jnp.exp(math.log(0.49536) - 2.30258505 * jax.random.uniform(splits[16], (D, D), jnp.float32) ** levels(splits[16], (D, D), ((0, 32),), -0.2, 0.2)), 0.049536, 0.49536)
    second_expand = jnp.clip(jnp.exp(math.log(4.9536) - 2.3025851 * jax.random.uniform(splits[17], (D, FF), jnp.float32) ** levels(splits[17], (D, FF), ((0, 32),), -0.2, 0.2)), 0.49536, 4.9536)
    second_reduce = jnp.clip(jnp.exp(math.log(16.512) - 2.30258501 * jax.random.uniform(splits[18], (FF, D), jnp.float32) ** levels(splits[18], (FF, D), ((0, 32),), -0.2, 0.2)), 1.6512, 16.512)
    second_vectors = jnp.clip(jnp.exp(math.log(49.536) - 2.3025851 * jax.random.uniform(splits[19], (NVEC, D), jnp.float32) ** levels(splits[19], (NVEC, D), ((1, 32),), -0.2, 0.2)), 4.9536, 49.536)
    second_bias = jnp.clip(jnp.exp(math.log(4.9536) - 2.3025851 * jax.random.uniform(splits[20], (FF,), jnp.float32) ** levels(splits[20], (FF,), ((0, 32),), -0.2, 0.2)), 0.49536, 4.9536)
    return {"tokens": tokens, "cotangent": cotangent, "lengths": lengths, "joint_weight": joint_weight, "output_weight": output_weight, "expand_weight": expand_weight, "reduce_weight": reduce_weight, "vectors": vectors, "expand_bias": expand_bias, "first_joint": first_joint, "first_output": first_output, "first_expand": first_expand, "first_reduce": first_reduce, "first_vectors": first_vectors, "first_bias": first_bias, "second_joint": second_joint, "second_output": second_output, "second_expand": second_expand, "second_reduce": second_reduce, "second_vectors": second_vectors, "second_bias": second_bias}


@jax.custom_vjp
def low(v):
    return lax.optimization_barrier(v.astype(jnp.bfloat16)).astype(jnp.float32)

@jax.custom_vjp
def low_back(v):
    return v

def low_keep(v):
    return (low(v), None)

def low_pass(kept, grad):
    return (grad,)

def back_keep(v):
    return (v, None)

def back_low(kept, grad):
    return (low(grad),)
low.defvjp(low_keep, low_pass)
low_back.defvjp(back_keep, back_low)
EPS_NORM = 1e-06
MASK_LOW = -1e+30
BETA_ONE = 0.9
BETA_TWO = 0.999
EPS_ADAM = 1e-08
STEP_RATES = (0.006, 0.05, 0.006, 0.004, 0.15, 0.02)
DECAY_RATES = (0.04, 0.04, 0.04, 0.04, 0.0, 0.0)

def norm_apply(features, gain_row, shift_row):
    average = lax.optimization_barrier(jnp.mean(features, axis=-1, keepdims=True))
    centered = features - average
    spread = lax.optimization_barrier(jnp.mean(centered * centered, axis=-1, keepdims=True))
    return centered * lax.rsqrt(spread + EPS_NORM) * gain_row + shift_row

def matmul(left, right):
    return jnp.dot(left, right, precision=lax.Precision.HIGHEST, preferred_element_type=jnp.float32)

def attend_image(pieces):
    grouped, valid_len = pieces
    queries = grouped[:, 0]
    key_rows = grouped[:, 1]
    value_rows = grouped[:, 2]
    raw_scores = jnp.einsum('qhd,khd->hqk', queries, key_rows, precision=lax.Precision.HIGHEST) * 0.125
    scores = low_back(raw_scores)
    usable = jnp.arange(L) < valid_len
    scores = jnp.where(usable[None, None, :], scores, MASK_LOW)
    highest = lax.optimization_barrier(jnp.max(scores, axis=-1, keepdims=True))
    exponent = jnp.exp(scores - highest)
    softmax = exponent / lax.optimization_barrier(jnp.sum(exponent, axis=-1, keepdims=True))
    attended = jnp.einsum('hqk,khd->qhd', low(softmax), value_rows, precision=lax.Precision.HIGHEST)
    return attended.reshape(L, H * HD)

def layer(token_arg, length_arg, joint_w, output_w, expand_w, reduce_w, vector_arg, bias_arg):
    normed = low(norm_apply(token_arg, vector_arg[0], vector_arg[1]))
    joint_bias = jnp.concatenate([vector_arg[2], jnp.zeros_like(vector_arg[2]), vector_arg[3]])
    joint = low_back(low(matmul(normed, joint_w) + joint_bias))
    grouped = joint.reshape(token_arg.shape[0], L, 3, H, HD)
    attended = lax.map(jax.checkpoint(attend_image), (grouped, length_arg))
    attended = low_back(low(attended))
    projected = low_back(matmul(attended, output_w) + vector_arg[4])
    hidden_one = token_arg + vector_arg[5] * projected
    normed_two = low(norm_apply(hidden_one, vector_arg[6], vector_arg[7]))
    expanded = low_back(matmul(normed_two, expand_w) + bias_arg)
    activated = low(jax.nn.gelu(expanded, approximate=False))
    reduced = low_back(matmul(activated, reduce_w) + vector_arg[8])
    return hidden_one + vector_arg[9] * reduced

def adam_update(weight, gradient, moment_one, moment_two, step_rate, decay_rate):
    mean_new = BETA_ONE * moment_one + (1.0 - BETA_ONE) * gradient
    square_new = BETA_TWO * moment_two + (1.0 - BETA_TWO) * gradient * gradient
    mean_hat = mean_new / (1.0 - BETA_ONE ** ADAM_STEP)
    square_hat = square_new / (1.0 - BETA_TWO ** ADAM_STEP)
    weight_f = weight.astype(jnp.float32)
    updated = weight_f - step_rate * (mean_hat / (jnp.sqrt(square_hat) + EPS_ADAM) + decay_rate * weight_f)
    return (updated, mean_new, square_new)

def reference(tokens, cotangent, lengths, joint_weight, output_weight, expand_weight, reduce_weight, vectors, expand_bias, first_joint, first_output, first_expand, first_reduce, first_vectors, first_bias, second_joint, second_output, second_expand, second_reduce, second_vectors, second_bias):
    params = tuple((weight.astype(jnp.float32) for weight in (joint_weight, output_weight, expand_weight, reduce_weight, vectors, expand_bias)))
    pairs = IMAGES // 2
    token_groups = tokens.astype(jnp.float32).reshape(pairs, 2, L, D)
    cot_groups = cotangent.astype(jnp.float32).reshape(pairs, 2, L, D)
    len_groups = lengths.astype(jnp.int32).reshape(pairs, 2)

    def group_step(summed, pieces):
        token_pair, cot_pair, len_pair = pieces

        def forward(token_arg, joint_w, output_w, expand_w, reduce_w, vector_arg, bias_arg):
            return layer(token_arg, len_pair, joint_w, output_w, expand_w, reduce_w, vector_arg, bias_arg)
        result, pullback = jax.vjp(forward, token_pair, params[0], params[1], params[2], params[3], params[4], params[5])
        usable = (jnp.arange(L)[None, :] < len_pair[:, None]).astype(jnp.float32)
        gradients = pullback(cot_pair * usable[:, :, None])
        summed = tuple((running + gradient for running, gradient in zip(summed, gradients[1:])))
        return (summed, (result.astype(jnp.bfloat16), gradients[0].astype(jnp.bfloat16)))
    start = tuple((jnp.zeros_like(weight) for weight in params))
    summed, outputs = lax.scan(group_step, start, (token_groups, cot_groups, len_groups))
    block_output = outputs[0].reshape(IMAGES, L, D)
    input_grad = outputs[1].reshape(IMAGES, L, D)
    firsts = (first_joint, first_output, first_expand, first_reduce, first_vectors, first_bias)
    seconds = (second_joint, second_output, second_expand, second_reduce, second_vectors, second_bias)
    raw_params = (joint_weight, output_weight, expand_weight, reduce_weight, vectors, expand_bias)
    updates = [adam_update(raw_params[index], summed[index], firsts[index], seconds[index], STEP_RATES[index], DECAY_RATES[index]) for index in range(6)]
    return (block_output, input_grad, summed[0], summed[1], summed[2], summed[3], summed[4], summed[5], updates[0][0], updates[1][0], updates[2][0], updates[3][0], updates[4][0], updates[5][0], updates[0][1], updates[1][1], updates[2][1], updates[3][1], updates[4][1], updates[5][1], updates[0][2], updates[1][2], updates[2][2], updates[3][2], updates[4][2], updates[5][2])
```

```python
import jax
import jax.numpy as jnp
from jax import lax
from jax.experimental import pallas as pl
from jax.experimental.pallas import tpu as pltpu
from jax.sharding import PartitionSpec as P

H = 16
HD = 64
ADAM_STEP = 2

EPS_NORM = 1e-06
MASK_LOW = -1e30
BETA_ONE = 0.9
BETA_TWO = 0.999
EPS_ADAM = 1e-08
STEP_RATES = (0.006, 0.05, 0.006, 0.004, 0.15, 0.02)
DECAY_RATES = (0.04, 0.04, 0.04, 0.04, 0.0, 0.0)
BOTH = ("seq", "fsdp")
F32 = jnp.float32
BF16 = jnp.bfloat16


def norm_apply(features, gain_row, shift_row):
    average = jnp.mean(features, axis=-1, keepdims=True)
    centered = features - average
    spread = jnp.mean(centered * centered, axis=-1, keepdims=True)
    return centered * lax.rsqrt(spread + EPS_NORM) * gain_row + shift_row


def gelu_parts(values):
    cdf = 0.5 * (1.0 + lax.erf(values * 0.7071067811865476))
    slope = cdf + values * (0.3989422804014327 * jnp.exp(-0.5 * values * values))
    return values * cdf, slope


def dot(left, right):
    return jnp.dot(left, right, preferred_element_type=F32)


def dot_rows(left, right):
    return lax.dot_general(left, right, (((0,), (0,)), ((), ())), preferred_element_type=F32)


def dot_t(left, right):
    return lax.dot_general(left, right, (((1,), (1,)), ((), ())), preferred_element_type=F32)


def pick(stack, index):
    return lax.dynamic_index_in_dim(stack, index, 0, keepdims=False)


def place(stack, piece, index):
    return lax.dynamic_update_index_in_dim(stack, piece, index, 0)


def shift_pairs(count, step):
    return [(i, (i + step) % count) for i in range(count)]


def gather_ring(piece, axis, count):
    me = lax.axis_index(axis)
    out = place(jnp.zeros((count,) + piece.shape, piece.dtype), piece, me)
    for step in range(1, count):
        got = lax.ppermute(piece, axis, shift_pairs(count, step))
        out = place(out, got, (me - step) % count)
    return out


def scatter_sum(parts, axis, count):
    me = lax.axis_index(axis)
    total = pick(parts, me)
    for step in range(1, count):
        sent = pick(parts, (me + step) % count)
        total = total + lax.ppermute(sent, axis, shift_pairs(count, step))
    return total


def gather_plane(piece, count):
    if count != 8:
        return lax.all_gather(piece, "seq", axis=0)
    me = lax.axis_index("seq")
    first = jnp.where(me % 2 == 0, 2, 4)
    second = 6 - first
    pairs_one = [(i, i ^ (2 if i % 2 == 0 else 4)) for i in range(8)]
    pairs_two = [(i, i ^ (4 if i % 2 == 0 else 2)) for i in range(8)]
    pairs_core = [(i, i ^ 1) for i in range(8)]
    one = lax.ppermute(piece, "seq", pairs_one)
    two = lax.ppermute(piece, "seq", pairs_two)
    three = lax.ppermute(one, "seq", pairs_two)
    mine = ((piece, me), (one, me ^ first), (two, me ^ second), (three, me ^ 6))
    theirs = (me ^ 1, me ^ 1 ^ second, me ^ 1 ^ first, me ^ 7)
    out = jnp.zeros((8,) + piece.shape, piece.dtype)
    for (block, index), other in zip(mine, theirs):
        out = place(out, block, index)
        out = place(out, lax.ppermute(block, "seq", pairs_core), other)
    return out


def head_lanes(shape, head):
    lane = lax.broadcasted_iota(jnp.int32, shape, len(shape) - 1)
    inside = (lane >= head * HD) & (lane < (head + 1) * HD)
    spare = lane == (HD if head == 0 else 0)
    return inside, spare


def attend_fwd_kernel(lens_ref, pos_ref, joint_ref, out_ref, q_scr, k_scr, v_scr, o_scr, *, heads, block):
    rows, width = o_scr.shape
    image = pl.program_id(0)

    def part(index):
        return joint_ref[:, 0, :, index * width : (index + 1) * width].reshape(rows, width)

    queries = part(0).astype(F32) * 0.125
    key_rows = part(1).astype(F32)
    v_scr[...] = part(2)
    bias = jnp.where(pos_ref[...] < lens_ref[image], 0.0, MASK_LOW)
    for head in range(heads):
        inside, spare = head_lanes((rows, width), head)
        q_scr[head] = jnp.where(inside, queries, jnp.where(spare, 1.0, 0.0)).astype(BF16)
        k_scr[head] = jnp.where(inside, key_rows, jnp.where(spare, bias, 0.0)).astype(BF16)

    def step(index, carry):
        start = pl.multiple_of(index * block, 16)
        value = None
        for head in range(heads):
            scores = dot_t(q_scr[head, pl.ds(start, block), :], k_scr[head])
            highest = jnp.max(scores, axis=1, keepdims=True)
            exponent = jnp.exp(scores - highest)
            inverse = 1.0 / jnp.sum(exponent, axis=1, keepdims=True)
            probs = (exponent * inverse).astype(BF16)
            result = dot(probs, v_scr[...])
            if head == 0:
                value = result
            else:
                inside, _ = head_lanes((block, width), head)
                value = jnp.where(inside, result, value)
        o_scr[pl.ds(start, block), :] = value
        return carry

    lax.fori_loop(0, rows // block, step, 0)
    out_ref[:, 0] = o_scr[...].astype(BF16).reshape(out_ref.shape[0], out_ref.shape[2], width)


def attend_bwd_kernel(
    lens_ref, pos_ref, joint_ref, grad_ref, out_ref, q_scr, k_scr, v_scr, g_scr, dq_scr, dk_scr, dv_scr, *, heads, block
):
    rows, width = v_scr.shape
    image = pl.program_id(0)

    def part(index):
        return joint_ref[:, 0, :, index * width : (index + 1) * width].reshape(rows, width)

    queries = part(0).astype(F32) * 0.125
    key_rows = part(1).astype(F32)
    grads = grad_ref[:, 0].reshape(rows, width).astype(F32)
    v_scr[...] = part(2)
    bias = jnp.where(pos_ref[...] < lens_ref[image], 0.0, MASK_LOW)
    for head in range(heads):
        inside, spare = head_lanes((rows, width), head)
        q_scr[head] = jnp.where(inside, queries, 0.0).astype(BF16)
        g_scr[head] = jnp.where(inside, grads, 0.0).astype(BF16)
        k_scr[head] = jnp.where(inside, key_rows, jnp.where(spare, bias, 0.0)).astype(BF16)
    dk_scr[...] = jnp.zeros_like(dk_scr)
    dv_scr[...] = jnp.zeros_like(dv_scr)

    def tile(start, size):
        dq = None
        dk = None
        dv = None
        for head in range(heads):
            _, spare = head_lanes((size, width), head)
            q_tile = q_scr[head, pl.ds(start, size), :]
            g_tile = g_scr[head, pl.ds(start, size), :]
            q_mask = jnp.where(spare, 1.0, q_tile.astype(F32)).astype(BF16)
            scores = dot_t(k_scr[head], q_mask)
            highest = jnp.max(scores, axis=0, keepdims=True)
            exponent = jnp.exp(scores - highest)
            probs = exponent * (1.0 / jnp.sum(exponent, axis=0, keepdims=True))
            grad_probs = dot_t(v_scr[...], g_tile)
            inner = jnp.sum(probs * grad_probs, axis=0, keepdims=True)
            grad_scores = (probs * (grad_probs - inner)).astype(BF16)
            dv_h = dot(probs.astype(BF16), g_tile)
            dk_h = dot(grad_scores, q_tile)
            dq_h = dot_rows(grad_scores, k_scr[head])
            dq = dq_h if dq is None else dq + dq_h
            dk = dk_h if dk is None else dk + dk_h
            dv = dv_h if dv is None else dv + dv_h
        dq_scr[pl.ds(start, size), :] = dq * 0.125
        dk_scr[...] += dk
        dv_scr[...] += dv

    def step(index, carry):
        tile(pl.multiple_of(index * block, 16), block)
        return carry

    whole = rows // block
    lax.fori_loop(0, whole, step, 0)
    if rows % block:
        tile(whole * block, rows % block)
    for index, grad in enumerate((dq_scr, dk_scr, dv_scr)):
        out_ref[:, 0, :, index * width : (index + 1) * width] = (
            grad[...].astype(BF16).reshape(out_ref.shape[0], out_ref.shape[2], width)
        )


def attend_specs(shape, width):
    parts, _, length, _ = shape
    rows = parts * length
    pos_spec = pl.BlockSpec((rows, width), lambda i, lens: (0, 0))

    def wide(count):
        return pl.BlockSpec((parts, 1, length, count * width), lambda i, lens: (0, i, 0, 0))

    return rows, pos_spec, wide


def attend_forward(joint, lengths, positions, heads, width):
    rows, pos_spec, wide = attend_specs(joint.shape, width)
    images = joint.shape[1]
    block = rows // 4

    def kernel(*refs):
        attend_fwd_kernel(*refs, heads=heads, block=block)

    return pl.pallas_call(
        kernel,
        out_shape=jax.ShapeDtypeStruct(joint.shape[:3] + (width,), BF16),
        grid_spec=pltpu.PrefetchScalarGridSpec(
            num_scalar_prefetch=1,
            grid=(images,),
            in_specs=[pos_spec, wide(3)],
            out_specs=wide(1),
            scratch_shapes=[
                pltpu.VMEM((heads, rows, width), BF16),
                pltpu.VMEM((heads, rows, width), BF16),
                pltpu.VMEM((rows, width), BF16),
                pltpu.VMEM((rows, width), F32),
            ],
        ),
        name="attend_forward",
    )(lengths, positions, joint)


def attend_backward(joint, grads, lengths, positions, heads, width):
    rows, pos_spec, wide = attend_specs(joint.shape, width)
    images = joint.shape[1]

    def kernel(*refs):
        attend_bwd_kernel(*refs, heads=heads, block=256)

    return pl.pallas_call(
        kernel,
        out_shape=jax.ShapeDtypeStruct(joint.shape, BF16),
        grid_spec=pltpu.PrefetchScalarGridSpec(
            num_scalar_prefetch=1,
            grid=(images,),
            in_specs=[pos_spec, wide(3), wide(1)],
            out_specs=wide(3),
            scratch_shapes=[
                pltpu.VMEM((heads, rows, width), BF16),
                pltpu.VMEM((heads, rows, width), BF16),
                pltpu.VMEM((rows, width), BF16),
                pltpu.VMEM((heads, rows, width), BF16),
                pltpu.VMEM((rows, width), F32),
                pltpu.VMEM((rows, width), F32),
                pltpu.VMEM((rows, width), F32),
            ],
        ),
        name="attend_backward",
    )(lengths, positions, joint, grads)


def adam_update(weight, gradient, moment_one, moment_two, step_rate, decay_rate):
    mean_new = BETA_ONE * moment_one + (1.0 - BETA_ONE) * gradient
    square_new = BETA_TWO * moment_two + (1.0 - BETA_TWO) * gradient * gradient
    mean_hat = mean_new / (1.0 - BETA_ONE**ADAM_STEP)
    square_hat = square_new / (1.0 - BETA_TWO**ADAM_STEP)
    weight_f = weight.astype(F32)
    updated = weight_f - step_rate * (
        mean_hat / (jnp.sqrt(square_hat) + EPS_ADAM) + decay_rate * weight_f
    )
    return (updated, mean_new, square_new)


def make_body(ns, nf):
    def body(
        tokens,
        cotangent,
        lengths,
        joint_weight,
        output_weight,
        expand_weight,
        reduce_weight,
        vectors,
        expand_bias,
        *moments,
    ):
        images, local_len, width = tokens.shape
        pad_len = -(-local_len // 16) * 16
        rows = images * pad_len
        heads = H // ns
        own = heads * HD
        lanes = max(own, 128)
        hidden = expand_weight.shape[1]
        slice_ff = hidden // ns
        seq = lax.axis_index("seq")

        def padded(array):
            array = jnp.pad(array, ((0, 0), (0, pad_len - local_len), (0, 0)))
            return array.reshape(rows, width)

        def unpadded(array):
            return array.reshape(images, pad_len, width)[:, :local_len]

        vector_rows = lax.all_gather(vectors, BOTH, axis=1, tiled=True).astype(F32)
        full_bias = lax.all_gather(expand_bias, BOTH, axis=0, tiled=True).astype(F32)

        features = padded(tokens).astype(F32)
        normed, norm_one_back = jax.vjp(norm_apply, features, vector_rows[0], vector_rows[1])
        normed_low = normed.astype(BF16)
        normed_all = gather_plane(normed_low, ns).reshape(ns * rows, width)

        own_rows = joint_weight.shape[0]
        pieces = joint_weight.reshape(own_rows, 3, ns, own).transpose(2, 0, 1, 3)
        pieces = lax.all_to_all(pieces, "seq", split_axis=0, concat_axis=0, tiled=True)
        pieces = gather_ring(pieces, "fsdp", nf)
        joint_own = pieces.transpose(1, 0, 2, 3, 4).reshape(width, 3, own)
        bias_own = lax.dynamic_slice_in_dim(vector_rows[2:4], seq * own, own, axis=1)
        bias_own = jnp.stack([bias_own[0], jnp.zeros_like(bias_own[0]), bias_own[1]])
        if lanes > own:
            joint_own = jnp.pad(joint_own, ((0, 0), (0, 0), (0, lanes - own)))
            bias_own = jnp.pad(bias_own, ((0, 0), (0, lanes - own)))
        joint = dot(normed_all, joint_own.reshape(width, 3 * lanes)) + bias_own.reshape(-1)
        joint = joint.astype(BF16).reshape(ns, images, pad_len, 3 * lanes)

        slot = jnp.arange(pad_len)
        live = (slot[None, :] < local_len) & (seq * local_len + slot[None, :] < lengths[:, None])
        grad_rows = padded(cotangent).astype(F32) * live.astype(F32).reshape(rows, 1)
        grad_reduced = (grad_rows * vector_rows[9]).astype(BF16)

        full_output = lax.all_gather(output_weight, BOTH, axis=0, tiled=True)
        full_expand = lax.all_gather(expand_weight, BOTH, axis=0, tiled=True)
        full_reduce = lax.all_gather(reduce_weight, BOTH, axis=0, tiled=True)
        grad_reduced_all = lax.all_gather(grad_reduced, "seq", axis=0, tiled=True)

        index = jnp.arange(ns * pad_len)
        position = jnp.where(
            index % pad_len < local_len, (index // pad_len) * local_len + index % pad_len, 1 << 30
        ).astype(jnp.int32)
        positions = jnp.broadcast_to(position[:, None], (ns * pad_len, lanes))
        attended = attend_forward(joint, lengths, positions, heads, lanes)
        attended_own = attended.reshape(ns, rows, lanes)[:, :, :own]
        attended_tok = lax.all_to_all(attended_own, "seq", split_axis=0, concat_axis=0, tiled=True)
        attended_rows = attended_tok.transpose(1, 0, 2).reshape(rows, width)

        projected = dot(attended_rows, full_output) + vector_rows[4]
        hidden_one = features + vector_rows[5] * projected
        normed_two, norm_two_back = jax.vjp(norm_apply, hidden_one, vector_rows[6], vector_rows[7])
        normed_two_low = normed_two.astype(BF16)
        normed_two_all = lax.all_gather(normed_two_low, "seq", axis=0, tiled=True)
        expanded = dot(normed_two_low, full_expand) + full_bias
        activated, slope = gelu_parts(expanded)
        reduced = dot(activated.astype(BF16), full_reduce) + vector_rows[8]
        block_output = unpadded((hidden_one + vector_rows[9] * reduced).astype(BF16))

        grad_scale_two = jnp.sum(grad_rows * reduced, axis=0)
        grad_reduce_bias = jnp.sum(grad_reduced.astype(F32), axis=0)
        grad_expanded = (dot_t(grad_reduced, full_reduce) * slope).astype(BF16)
        grad_normed_two = dot_t(grad_expanded, full_expand)
        grad_hidden_part, grad_gain_two, grad_shift_two = norm_two_back(grad_normed_two)
        grad_hidden = grad_rows + grad_hidden_part
        grad_scale_one = jnp.sum(grad_hidden * projected, axis=0)
        grad_projected = (grad_hidden * vector_rows[5]).astype(BF16)
        grad_output_bias = jnp.sum(grad_projected.astype(F32), axis=0)
        grad_attended = dot_t(grad_projected, full_output).astype(BF16)
        grad_attended = grad_attended.reshape(rows, ns, own).transpose(1, 0, 2)
        grad_heads = lax.all_to_all(grad_attended, "seq", split_axis=0, concat_axis=0, tiled=True)
        grad_projected_all = lax.all_gather(grad_projected, "seq", axis=0, tiled=True)
        if lanes > own:
            grad_heads = jnp.pad(grad_heads, ((0, 0), (0, 0), (0, lanes - own)))
        grad_heads = grad_heads.reshape(ns, images, pad_len, lanes)

        expand_own = lax.dynamic_slice_in_dim(full_expand, seq * slice_ff, slice_ff, axis=1)
        reduce_own = lax.dynamic_slice_in_dim(full_reduce, seq * slice_ff, slice_ff, axis=0)
        ff_bias_own = lax.dynamic_slice_in_dim(full_bias, seq * slice_ff, slice_ff, axis=0)
        expanded_own = dot(normed_two_all, expand_own) + ff_bias_own
        activated_own, slope_own = gelu_parts(expanded_own)
        grad_expanded_own = (dot_t(grad_reduced_all, reduce_own) * slope_own).astype(BF16)
        part_reduce = dot_rows(activated_own.astype(BF16), grad_reduced_all)
        part_expand = dot_rows(normed_two_all, grad_expanded_own)
        part_bias = jnp.sum(grad_expanded_own.astype(F32), axis=0)
        own_reduce = scatter_sum(part_reduce.reshape(nf, -1, width), "fsdp", nf)
        own_expand = scatter_sum(
            part_expand.reshape(ns, nf, own_rows, slice_ff).transpose(1, 0, 2, 3), "fsdp", nf
        )
        own_expand = lax.all_to_all(own_expand, "seq", split_axis=0, concat_axis=0, tiled=True)
        own_expand = own_expand.transpose(1, 0, 2).reshape(own_rows, hidden)
        own_bias = scatter_sum(part_bias.reshape(nf, -1), "fsdp", nf)

        grad_joint = attend_backward(joint, grad_heads, lengths, positions, heads, lanes)
        part_output = dot_rows(attended_own.reshape(ns * rows, own), grad_projected_all)
        own_output = scatter_sum(part_output.reshape(nf, -1, width), "fsdp", nf)
        grad_joint_own = grad_joint.reshape(ns * rows, 3, lanes)[:, :, :own].reshape(ns, rows, 3 * own)
        grad_joint_flat = grad_joint_own.reshape(ns * rows, 3 * own)
        part_joint = dot_rows(normed_all, grad_joint_flat)
        joint_sums = jnp.sum(grad_joint_flat.astype(F32), axis=0)
        own_joint = scatter_sum(
            part_joint.reshape(ns, nf, own_rows, 3 * own).transpose(1, 0, 2, 3), "fsdp", nf
        )
        own_joint = lax.all_to_all(own_joint, "seq", split_axis=0, concat_axis=0, tiled=True)
        own_joint = own_joint.reshape(ns, own_rows, 3, own).transpose(1, 2, 0, 3).reshape(own_rows, 3 * width)

        full_joint = lax.all_gather(joint_weight, BOTH, axis=0, tiled=True)
        grad_tok = lax.all_to_all(grad_joint_own, "seq", split_axis=0, concat_axis=0, tiled=True)
        grad_tok = grad_tok.reshape(ns, rows, 3, own).transpose(1, 2, 0, 3).reshape(rows, 3 * width)
        grad_normed = dot_t(grad_tok, full_joint)
        grad_input_part, grad_gain_one, grad_shift_one = norm_one_back(grad_normed)
        input_grad = unpadded((grad_hidden + grad_input_part).astype(BF16))

        token_sums = jnp.stack(
            [
                grad_gain_one,
                grad_shift_one,
                grad_output_bias,
                grad_scale_one,
                grad_gain_two,
                grad_shift_two,
                grad_reduce_bias,
                grad_scale_two,
            ]
        )
        token_sums = token_sums.reshape(8, ns, own).transpose(1, 0, 2)
        plane_sums = pick(token_sums, seq)
        for step in range(1, ns):
            sent = pick(token_sums, (seq + step) % ns)
            plane_sums = plane_sums + lax.ppermute(sent, "seq", shift_pairs(ns, step))
        plane_sums = jnp.concatenate(
            [plane_sums[:2], joint_sums[None, :own], joint_sums[None, 2 * own :], plane_sums[2:]]
        )
        own_vectors = scatter_sum(plane_sums.reshape(10, nf, -1).transpose(1, 0, 2), "fsdp", nf)

        owned = (own_joint, own_output, own_expand, own_reduce, own_vectors, own_bias)
        shards = (joint_weight, output_weight, expand_weight, reduce_weight, vectors, expand_bias)
        updates = [
            adam_update(
                shards[i], owned[i], moments[i], moments[6 + i], STEP_RATES[i], DECAY_RATES[i]
            )
            for i in range(6)
        ]
        return (
            block_output,
            input_grad,
            *owned,
            *(u[0] for u in updates),
            *(u[1] for u in updates),
            *(u[2] for u in updates),
        )

    return body


def solution(mesh):
    by_token = P("fsdp", "seq", None)
    by_row = P(BOTH, None)
    six = (by_row, by_row, by_row, by_row, P(None, BOTH), P(BOTH))
    return jax.shard_map(
        make_body(mesh.shape["seq"], mesh.shape["fsdp"]),
        mesh=mesh,
        in_specs=(by_token, by_token, P("fsdp")) + six * 3,
        out_specs=(by_token, by_token) + six * 4,
        check_vma=False,
    )
```

```python
import jax
import jax.numpy as jnp
from jax import lax
from jax.experimental import pallas as pl
from jax.experimental.pallas import tpu as pltpu
from jax.sharding import PartitionSpec as P

H = 16
HD = 64
ADAM_STEP = 2

EPS_NORM = 1e-06
MASK_LOW = -1e30
BETA_ONE = 0.9
BETA_TWO = 0.999
EPS_ADAM = 1e-08
STEP_RATES = (0.006, 0.05, 0.006, 0.004, 0.15, 0.02)
DECAY_RATES = (0.04, 0.04, 0.04, 0.04, 0.0, 0.0)
BOTH = ("seq", "fsdp")
F32 = jnp.float32
BF16 = jnp.bfloat16


def norm_apply(features, gain_row, shift_row):
    average = jnp.mean(features, axis=-1, keepdims=True)
    centered = features - average
    spread = jnp.mean(centered * centered, axis=-1, keepdims=True)
    return centered * lax.rsqrt(spread + EPS_NORM) * gain_row + shift_row


def gelu_parts(values):
    cdf = 0.5 * (1.0 + lax.erf(values * 0.7071067811865476))
    slope = cdf + values * (0.3989422804014327 * jnp.exp(-0.5 * values * values))
    return values * cdf, slope


def dot(left, right):
    return jnp.dot(left, right, preferred_element_type=F32)


def dot_rows(left, right):
    return lax.dot_general(left, right, (((0,), (0,)), ((), ())), preferred_element_type=F32)


def dot_t(left, right):
    return lax.dot_general(left, right, (((1,), (1,)), ((), ())), preferred_element_type=F32)


def pick(stack, index, axis=0):
    return lax.dynamic_index_in_dim(stack, index, axis, keepdims=False)


def place(stack, piece, index):
    return lax.dynamic_update_index_in_dim(stack, piece, index, 0)


def shift_pairs(count, step):
    return [(i, (i + step) % count) for i in range(count)]


def gather_ring(piece, axis, count):
    me = lax.axis_index(axis)
    out = jnp.broadcast_to(piece[None], (count,) + piece.shape)
    for step in range(1, count):
        got = lax.ppermute(piece, axis, shift_pairs(count, step))
        out = place(out, got, (me - step) % count)
    return out


def scatter_sum(parts, axis, count, dim=0):
    me = lax.axis_index(axis)
    total = pick(parts, me, dim)
    for step in range(1, count):
        sent = pick(parts, (me + step) % count, dim)
        total = total + lax.ppermute(sent, axis, shift_pairs(count, step))
    return total


def swap(array):
    return lax.all_to_all(array, "seq", split_axis=0, concat_axis=0, tiled=True)


def side_by_side(blocks, start, size):
    return [blocks[i, :, start : start + size] for i in range(blocks.shape[0])]


def gather_plane(piece, count):
    if count != 8:
        return lax.all_gather(piece, "seq", axis=0)
    me = lax.axis_index("seq")
    first = jnp.where(me % 2 == 0, 2, 4)
    second = 6 - first
    pairs_one = [(i, i ^ (2 if i % 2 == 0 else 4)) for i in range(8)]
    pairs_two = [(i, i ^ (4 if i % 2 == 0 else 2)) for i in range(8)]
    pairs_core = [(i, i ^ 1) for i in range(8)]
    one = lax.ppermute(piece, "seq", pairs_one)
    two = lax.ppermute(piece, "seq", pairs_two)
    three = lax.ppermute(one, "seq", pairs_two)
    mine = ((piece, me), (one, me ^ first), (two, me ^ second), (three, me ^ 6))
    theirs = (me ^ 1, me ^ 1 ^ second, me ^ 1 ^ first, me ^ 7)
    out = jnp.broadcast_to(piece[None], (8,) + piece.shape)
    for (block, index), other in zip(mine, theirs):
        if block is not piece:
            out = place(out, block, index)
        out = place(out, lax.ppermute(block, "seq", pairs_core), other)
    return out


def head_lanes(shape, head):
    lane = lax.broadcasted_iota(jnp.int32, shape, len(shape) - 1)
    inside = (lane >= head * HD) & (lane < (head + 1) * HD)
    spare = lane == (HD if head == 0 else 0)
    return inside, spare


def attend_fwd_kernel(lens_ref, pos_ref, joint_ref, out_ref, q_scr, k_scr, v_scr, o_scr, *, heads, block):
    rows, width = o_scr.shape
    image = pl.program_id(0)

    def part(index):
        return joint_ref[:, 0, :, index * width : (index + 1) * width].reshape(rows, width)

    queries = part(0).astype(F32) * 0.125
    key_rows = part(1).astype(F32)
    v_scr[...] = part(2)
    bias = jnp.where(pos_ref[...] < lens_ref[image], 0.0, MASK_LOW)
    for head in range(heads):
        inside, spare = head_lanes((rows, width), head)
        q_scr[head] = jnp.where(inside, queries, jnp.where(spare, 1.0, 0.0)).astype(BF16)
        k_scr[head] = jnp.where(inside, key_rows, jnp.where(spare, bias, 0.0)).astype(BF16)

    def step(index, carry):
        start = pl.multiple_of(index * block, 16)
        value = None
        for head in range(heads):
            scores = dot_t(q_scr[head, pl.ds(start, block), :], k_scr[head])
            highest = jnp.max(scores, axis=1, keepdims=True)
            exponent = jnp.exp(scores - highest)
            inverse = 1.0 / jnp.sum(exponent, axis=1, keepdims=True)
            probs = (exponent * inverse).astype(BF16)
            result = dot(probs, v_scr[...])
            if head == 0:
                value = result
            else:
                inside, _ = head_lanes((block, width), head)
                value = jnp.where(inside, result, value)
        o_scr[pl.ds(start, block), :] = value
        return carry

    lax.fori_loop(0, rows // block, step, 0)
    out_ref[:, 0] = o_scr[...].astype(BF16).reshape(out_ref.shape[0], out_ref.shape[2], width)


def attend_bwd_kernel(
    lens_ref, pos_ref, joint_ref, grad_ref, out_ref, q_scr, k_scr, v_scr, g_scr, dq_scr, dk_scr, dv_scr, *, heads, block
):
    rows, width = v_scr.shape
    image = pl.program_id(0)

    def part(index):
        return joint_ref[:, 0, :, index * width : (index + 1) * width].reshape(rows, width)

    queries = part(0).astype(F32) * 0.125
    key_rows = part(1).astype(F32)
    grads = grad_ref[:, 0].reshape(rows, width).astype(F32)
    v_scr[...] = part(2)
    bias = jnp.where(pos_ref[...] < lens_ref[image], 0.0, MASK_LOW)
    for head in range(heads):
        inside, spare = head_lanes((rows, width), head)
        q_scr[head] = jnp.where(inside, queries, 0.0).astype(BF16)
        g_scr[head] = jnp.where(inside, grads, 0.0).astype(BF16)
        k_scr[head] = jnp.where(inside, key_rows, jnp.where(spare, bias, 0.0)).astype(BF16)
    dk_scr[...] = jnp.zeros_like(dk_scr)
    dv_scr[...] = jnp.zeros_like(dv_scr)

    def tile(start, size):
        dq = None
        dk = None
        dv = None
        for head in range(heads):
            _, spare = head_lanes((size, width), head)
            q_tile = q_scr[head, pl.ds(start, size), :]
            g_tile = g_scr[head, pl.ds(start, size), :]
            q_mask = jnp.where(spare, 1.0, q_tile.astype(F32)).astype(BF16)
            scores = dot_t(k_scr[head], q_mask)
            highest = jnp.max(scores, axis=0, keepdims=True)
            exponent = jnp.exp(scores - highest)
            probs = exponent * (1.0 / jnp.sum(exponent, axis=0, keepdims=True))
            grad_probs = dot_t(v_scr[...], g_tile)
            inner = jnp.sum(probs * grad_probs, axis=0, keepdims=True)
            grad_scores = (probs * (grad_probs - inner)).astype(BF16)
            dv_h = dot(probs.astype(BF16), g_tile)
            dk_h = dot(grad_scores, q_tile)
            dq_h = dot_rows(grad_scores, k_scr[head])
            dq = dq_h if dq is None else dq + dq_h
            dk = dk_h if dk is None else dk + dk_h
            dv = dv_h if dv is None else dv + dv_h
        dq_scr[pl.ds(start, size), :] = dq * 0.125
        dk_scr[...] += dk
        dv_scr[...] += dv

    def step(index, carry):
        tile(pl.multiple_of(index * block, 16), block)
        return carry

    whole = rows // block
    lax.fori_loop(0, whole, step, 0)
    if rows % block:
        tile(whole * block, rows % block)
    for index, grad in enumerate((dq_scr, dk_scr, dv_scr)):
        out_ref[:, 0, :, index * width : (index + 1) * width] = (
            grad[...].astype(BF16).reshape(out_ref.shape[0], out_ref.shape[2], width)
        )


def attend_specs(shape, width):
    parts, _, length, _ = shape
    rows = parts * length
    pos_spec = pl.BlockSpec((rows, width), lambda i, lens: (0, 0))

    def wide(count):
        return pl.BlockSpec((parts, 1, length, count * width), lambda i, lens: (0, i, 0, 0))

    return rows, pos_spec, wide


def attend_forward(joint, lengths, positions, heads, width):
    rows, pos_spec, wide = attend_specs(joint.shape, width)
    images = joint.shape[1]
    block = rows // 4

    def kernel(*refs):
        attend_fwd_kernel(*refs, heads=heads, block=block)

    return pl.pallas_call(
        kernel,
        out_shape=jax.ShapeDtypeStruct(joint.shape[:3] + (width,), BF16),
        grid_spec=pltpu.PrefetchScalarGridSpec(
            num_scalar_prefetch=1,
            grid=(images,),
            in_specs=[pos_spec, wide(3)],
            out_specs=wide(1),
            scratch_shapes=[
                pltpu.VMEM((heads, rows, width), BF16),
                pltpu.VMEM((heads, rows, width), BF16),
                pltpu.VMEM((rows, width), BF16),
                pltpu.VMEM((rows, width), F32),
            ],
        ),
        name="attend_forward",
    )(lengths, positions, joint)


def attend_backward(joint, grads, lengths, positions, heads, width):
    rows, pos_spec, wide = attend_specs(joint.shape, width)
    images = joint.shape[1]

    def kernel(*refs):
        attend_bwd_kernel(*refs, heads=heads, block=256)

    return pl.pallas_call(
        kernel,
        out_shape=jax.ShapeDtypeStruct(joint.shape, BF16),
        grid_spec=pltpu.PrefetchScalarGridSpec(
            num_scalar_prefetch=1,
            grid=(images,),
            in_specs=[pos_spec, wide(3), wide(1)],
            out_specs=wide(3),
            scratch_shapes=[
                pltpu.VMEM((heads, rows, width), BF16),
                pltpu.VMEM((heads, rows, width), BF16),
                pltpu.VMEM((rows, width), BF16),
                pltpu.VMEM((heads, rows, width), BF16),
                pltpu.VMEM((rows, width), F32),
                pltpu.VMEM((rows, width), F32),
                pltpu.VMEM((rows, width), F32),
            ],
        ),
        name="attend_backward",
    )(lengths, positions, joint, grads)


def adam_update(weight, gradient, moment_one, moment_two, step_rate, decay_rate):
    mean_new = BETA_ONE * moment_one + (1.0 - BETA_ONE) * gradient
    square_new = BETA_TWO * moment_two + (1.0 - BETA_TWO) * gradient * gradient
    mean_hat = mean_new / (1.0 - BETA_ONE**ADAM_STEP)
    square_hat = square_new / (1.0 - BETA_TWO**ADAM_STEP)
    weight_f = weight.astype(F32)
    updated = weight_f - step_rate * (
        mean_hat / (jnp.sqrt(square_hat) + EPS_ADAM) + decay_rate * weight_f
    )
    return (updated, mean_new, square_new)


def make_body(ns, nf):
    def body(
        tokens,
        cotangent,
        lengths,
        joint_weight,
        output_weight,
        expand_weight,
        reduce_weight,
        vectors,
        expand_bias,
        *moments,
    ):
        images, local_len, width = tokens.shape
        pad_len = -(-local_len // 16) * 16
        rows = images * pad_len
        heads = H // ns
        own = heads * HD
        lanes = max(own, 128)
        hidden = expand_weight.shape[1]
        slice_ff = hidden // ns
        seq = lax.axis_index("seq")

        def padded(array):
            array = jnp.pad(array, ((0, 0), (0, pad_len - local_len), (0, 0)))
            return array.reshape(rows, width)

        def unpadded(array):
            return array.reshape(images, pad_len, width)[:, :local_len]

        vector_size = vectors.size
        small = jnp.concatenate([vectors.reshape(-1), expand_bias])
        small = gather_ring(gather_ring(small, "fsdp", nf), "seq", ns)
        vector_rows = small[:, :, :vector_size].reshape(ns, nf, vectors.shape[0], -1)
        vector_rows = vector_rows.transpose(2, 0, 1, 3).reshape(vectors.shape[0], width).astype(F32)
        full_bias = small[:, :, vector_size:].reshape(-1).astype(F32)

        features = padded(tokens).astype(F32)
        normed, norm_one_back = jax.vjp(norm_apply, features, vector_rows[0], vector_rows[1])
        normed_low = normed.astype(BF16).reshape(images, pad_len, width)
        normed_all = [
            gather_plane(normed_low[i], ns).reshape(ns * pad_len, width) for i in range(images)
        ]

        own_rows = joint_weight.shape[0]
        joint_z = gather_ring(joint_weight, "fsdp", nf).reshape(nf * own_rows, 3 * width)
        output_z = gather_ring(output_weight, "fsdp", nf).reshape(-1, width)
        expand_z = gather_ring(expand_weight, "fsdp", nf).reshape(-1, hidden)
        reduce_z = gather_ring(reduce_weight, "fsdp", nf).reshape(-1, width)
        pieces = jnp.stack(
            [
                jnp.concatenate(
                    [joint_z[:, c * width + j * own : c * width + (j + 1) * own] for c in range(3)], axis=1
                )
                for j in range(ns)
            ]
        )
        joint_own = swap(pieces).reshape(width, 3 * own)
        bias_own = lax.dynamic_slice_in_dim(vector_rows[2:4], seq * own, own, axis=1)
        bias_own = jnp.stack([bias_own[0], jnp.zeros_like(bias_own[0]), bias_own[1]])
        if lanes > own:
            joint_own = jnp.pad(joint_own.reshape(width, 3, own), ((0, 0), (0, 0), (0, lanes - own)))
            joint_own = joint_own.reshape(width, 3 * lanes)
            bias_own = jnp.pad(bias_own, ((0, 0), (0, lanes - own)))
        bias_own = bias_own.reshape(-1)

        slot = jnp.arange(pad_len)
        live = (slot[None, :] < local_len) & (seq * local_len + slot[None, :] < lengths[:, None])
        grad_rows = padded(cotangent).astype(F32) * live.astype(F32).reshape(rows, 1)
        grad_reduced = (grad_rows * vector_rows[9]).astype(BF16)

        full_expand = lax.all_gather(expand_z, "seq", axis=0, tiled=True)
        full_reduce = lax.all_gather(reduce_z, "seq", axis=0, tiled=True)
        full_output = gather_plane(output_z, ns).reshape(width, width)
        grad_reduced_all = lax.all_gather(grad_reduced, "seq", axis=0, tiled=True)

        index = jnp.arange(ns * pad_len)
        position = jnp.where(
            index % pad_len < local_len, (index // pad_len) * local_len + index % pad_len, 1 << 30
        ).astype(jnp.int32)
        positions = jnp.broadcast_to(position[:, None], (ns * pad_len, lanes))
        joint = []
        attended_own = []
        attended_rows = []
        for i in range(images):
            made = (dot(normed_all[i], joint_own) + bias_own).astype(BF16)
            joint.append(made.reshape(ns, 1, pad_len, 3 * lanes))
            attended = attend_forward(joint[i], lengths[i : i + 1], positions, heads, lanes)
            attended_own.append(attended.reshape(ns, pad_len, lanes)[:, :, :own])
            attended_rows.append(jnp.concatenate(side_by_side(swap(attended_own[i]), 0, own), axis=1))
        attended_rows = jnp.concatenate(attended_rows, axis=0)

        projected = dot(attended_rows, full_output) + vector_rows[4]
        hidden_one = features + vector_rows[5] * projected
        normed_two, norm_two_back = jax.vjp(norm_apply, hidden_one, vector_rows[6], vector_rows[7])
        normed_two_low = normed_two.astype(BF16)
        normed_two_all = lax.all_gather(normed_two_low, "seq", axis=0, tiled=True)
        expanded = dot(normed_two_low, full_expand) + full_bias
        activated, slope = gelu_parts(expanded)
        reduced = dot(activated.astype(BF16), full_reduce) + vector_rows[8]
        block_output = unpadded((hidden_one + vector_rows[9] * reduced).astype(BF16))

        grad_scale_two = jnp.sum(grad_rows * reduced, axis=0)
        grad_reduce_bias = jnp.sum(grad_reduced.astype(F32), axis=0)
        grad_expanded = (dot_t(grad_reduced, full_reduce) * slope).astype(BF16)
        grad_normed_two = dot_t(grad_expanded, full_expand)
        grad_hidden_part, grad_gain_two, grad_shift_two = norm_two_back(grad_normed_two)
        grad_hidden = grad_rows + grad_hidden_part
        grad_scale_one = jnp.sum(grad_hidden * projected, axis=0)
        grad_projected = (grad_hidden * vector_rows[5]).astype(BF16)
        grad_output_bias = jnp.sum(grad_projected.astype(F32), axis=0)
        grad_attended = dot_t(grad_projected, full_output).astype(BF16)
        grad_heads = []
        for i in range(images):
            part = grad_attended[i * pad_len : (i + 1) * pad_len]
            part = swap(jnp.stack([part[:, j * own : (j + 1) * own] for j in range(ns)]))
            if lanes > own:
                part = jnp.pad(part, ((0, 0), (0, 0), (0, lanes - own)))
            grad_heads.append(part.reshape(ns, 1, pad_len, lanes))
        grad_projected_all = lax.all_gather(
            grad_projected.reshape(images, pad_len, width), "seq", axis=0
        )

        expand_own = lax.dynamic_slice_in_dim(full_expand, seq * slice_ff, slice_ff, axis=1)
        ff_bias_own = lax.dynamic_slice_in_dim(full_bias, seq * slice_ff, slice_ff, axis=0)
        expanded_own = dot(normed_two_all, expand_own) + ff_bias_own
        activated_own, slope_own = gelu_parts(expanded_own)
        grad_expanded_own = (dot_t(grad_reduced_all, reduce_z) * slope_own).astype(BF16)
        part_reduce = dot_rows(activated_own.astype(BF16), grad_reduced_all)
        part_expand = dot_rows(normed_two_all, grad_expanded_own)
        part_bias = jnp.sum(grad_expanded_own.astype(F32), axis=0)
        grad_heads[0], part_reduce, part_expand = lax.optimization_barrier(
            (grad_heads[0], part_reduce, part_expand)
        )
        own_reduce = scatter_sum(part_reduce.reshape(nf, -1, width), "fsdp", nf)
        own_expand = scatter_sum(part_expand.reshape(ns, nf, own_rows, slice_ff), "fsdp", nf, 1)
        own_expand = jnp.concatenate(side_by_side(swap(own_expand), 0, slice_ff), axis=1)
        own_bias = scatter_sum(part_bias.reshape(nf, -1), "fsdp", nf)

        part_joint = 0.0
        part_output = 0.0
        joint_sums = 0.0
        grad_tok = []
        for i in range(images):
            made = attend_backward(joint[i], grad_heads[i], lengths[i : i + 1], positions, heads, lanes)
            made = made.reshape(ns, pad_len, 3 * lanes)
            if lanes > own:
                made = jnp.concatenate(
                    [made[:, :, c * lanes : c * lanes + own] for c in range(3)], axis=2
                )
            back = swap(made)
            grad_tok.append(
                jnp.concatenate(
                    [block for c in range(3) for block in side_by_side(back, c * own, own)], axis=1
                )
            )
            flat = made.reshape(ns * pad_len, 3 * own)
            part_joint = part_joint + dot_rows(normed_all[i], flat)
            joint_sums = joint_sums + jnp.sum(flat.astype(F32), axis=0)
        own_joint = scatter_sum(part_joint.reshape(ns, nf, own_rows, 3 * own), "fsdp", nf, 1)
        own_joint = swap(own_joint)
        own_joint = jnp.concatenate(
            [block for c in range(3) for block in side_by_side(own_joint, c * own, own)], axis=1
        )
        for i in range(images):
            part_output = part_output + dot_rows(
                attended_own[i].reshape(ns * pad_len, own),
                grad_projected_all[:, i].reshape(ns * pad_len, width),
            )
        own_output = scatter_sum(part_output.reshape(nf, -1, width), "fsdp", nf)

        full_joint = lax.all_gather(joint_z, "seq", axis=0, tiled=True)
        grad_normed = dot_t(jnp.concatenate(grad_tok, axis=0), full_joint)
        grad_input_part, grad_gain_one, grad_shift_one = norm_one_back(grad_normed)
        input_grad = unpadded((grad_hidden + grad_input_part).astype(BF16))

        def over_plane(sums):
            sums = jnp.stack(sums).reshape(len(sums), ns, own)
            return scatter_sum(sums, "seq", ns, 1)

        late = over_plane([grad_gain_one, grad_shift_one])
        early = over_plane(
            [
                grad_output_bias,
                grad_scale_one,
                grad_gain_two,
                grad_shift_two,
                grad_reduce_bias,
                grad_scale_two,
            ]
        )
        plane_sums = jnp.concatenate(
            [late, joint_sums[None, :own], joint_sums[None, 2 * own :], early]
        )
        own_vectors = scatter_sum(plane_sums.reshape(10, nf, -1).transpose(1, 0, 2), "fsdp", nf)

        owned = (own_joint, own_output, own_expand, own_reduce, own_vectors, own_bias)
        shards = (joint_weight, output_weight, expand_weight, reduce_weight, vectors, expand_bias)
        updates = [
            adam_update(
                shards[i], owned[i], moments[i], moments[6 + i], STEP_RATES[i], DECAY_RATES[i]
            )
            for i in range(6)
        ]
        return (
            block_output,
            input_grad,
            *owned,
            *(u[0] for u in updates),
            *(u[1] for u in updates),
            *(u[2] for u in updates),
        )

    return body


def solution(mesh):
    by_token = P("fsdp", "seq", None)
    by_row = P(BOTH, None)
    six = (by_row, by_row, by_row, by_row, P(None, BOTH), P(BOTH))
    return jax.shard_map(
        make_body(mesh.shape["seq"], mesh.shape["fsdp"]),
        mesh=mesh,
        in_specs=(by_token, by_token, P("fsdp")) + six * 3,
        out_specs=(by_token, by_token) + six * 4,
        check_vma=False,
    )
```
